32 devices in a mesh: row: 8 (over z, x), col: 4 (over y, core).
Axes of the slice: x: 2, y: 2, z: 4, core: 2. Of those that a mesh axis runs over, the one named last changes fastest.
Arguments:
- margin: bfloat16 [32, 128, 1152], P(('row', 'col')), may hold values from -0.2 to 1.2, as said below
- fock_matrix: bfloat16 [32, 128, 1152], P(('row', 'col')), may hold values from -0.4 to 0.4, as said below
- density: bfloat16 [32, 128, 1152], P(('row', 'col')), may hold values from -4 to 4, as said below
- present: int32 [32, 9], P(('row', 'col')), may hold values from 0 to 1, as said below
Outputs:
- gradient: float32 [32, 128, 1152], P(('row', 'col'))
- updated: float32 [32, 128, 1152], P(('row', 'col'))
The draws below stay inside these ranges and needn't reach their ends.
Inputs may be any that keep to these rules, and one draw needn't show every extreme that they name: present[r, 4] is 1; present[r, o + 4] equals present[r + o, 4 - o]; slots whose block lies outside the matrix are 0. `margin`: symmetric: block (r, o) is the transpose of block (r + o, -o); blocks where present is 0 are zero. `fock_matrix`: symmetric: block (r, o) is the transpose of block (r + o, -o); blocks where present is 0 are zero. `density`: symmetric: block (r, o) is the transpose of block (r + o, -o); blocks where present is 0 are zero.
All inputs are finite; a program needn't handle non-finite values.
Results may differ from the reference program's by a relative error of at most 0.0041.
Values may be sent and summed in bfloat16 or wider, within the bound.
A program may use at most 64 MiB of HBM per device.

```python
import jax
import jax.numpy as jnp
from jax import lax

BLOCK = 128
HALF_BAND = 4
BAND = 9
BLOCKS = 32


def pattern(key):
    random_bits = jax.random.randint(jax.random.fold_in(key, 11), (BLOCKS, HALF_BAND), 0, 4)
    upper_bits = (random_bits < 3).astype(jnp.int32)
    row_index = jnp.arange(BLOCKS, dtype=jnp.int32)
    columns = []
    for offset in range(-HALF_BAND, HALF_BAND + 1):
        if offset == 0:
            columns.append(jnp.ones((BLOCKS,), jnp.int32))
        elif offset > 0:
            columns.append(upper_bits[:, offset - 1] * (row_index + offset < BLOCKS).astype(jnp.int32))
        else:
            rolled = jnp.roll(upper_bits[:, -offset - 1], -offset)
            columns.append(rolled * (row_index + offset >= 0).astype(jnp.int32))
    return jnp.stack(columns, axis=1)


def symmetric(key, salt, factor):
    present = pattern(key)
    shape = (BLOCKS, BLOCK, BAND, BLOCK)
    random_draw = jnp.clip(jax.random.normal(jax.random.fold_in(key, salt), shape, jnp.float32), -4.0, 4.0)
    slot_list = []
    for offset in range(-HALF_BAND, HALF_BAND + 1):
        own_block = random_draw[:, :, HALF_BAND + offset, :]
        partner = jnp.roll(random_draw[:, :, HALF_BAND - offset, :], -offset, axis=0)
        slot_list.append(0.5 * (own_block + jnp.swapaxes(partner, 1, 2)))
    symmetrized = jnp.stack(slot_list, axis=2) * present.astype(jnp.float32)[:, None, :, None]
    return factor * symmetrized


def draw_present(key, part):
    return pattern(key)


def draw_margin(key, part):
    entry_scale = 0.4 * (BAND * BLOCK) ** (-0.5)
    values = symmetric(key, 21, entry_scale)
    identity = jnp.eye(BLOCK, dtype=jnp.float32)
    diagonal = jnp.zeros((BAND,), jnp.float32).at[HALF_BAND].set(1.0)
    values = values + identity[None, :, None, :] * diagonal[None, None, :, None]
    return values.reshape(BLOCKS, BLOCK, BAND * BLOCK).astype(jnp.bfloat16)


def draw_fock_matrix(key, part):
    entry_scale = (BAND * BLOCK) ** (-0.5)
    return symmetric(key, 33, entry_scale).reshape(BLOCKS, BLOCK, BAND * BLOCK).astype(jnp.bfloat16)


def draw_density(key, part):
    return symmetric(key, 45, 1.0).reshape(BLOCKS, BLOCK, BAND * BLOCK).astype(jnp.bfloat16)


def setup_inputs(seed: int = 0) -> dict:
    splits = jax.random.split(jax.random.key(seed), 5)
    margin = draw_margin(jax.random.fold_in(splits[4], 71), 0)
    fock_matrix = draw_fock_matrix(jax.random.fold_in(splits[4], 71), 0)
    density = draw_density(jax.random.fold_in(splits[4], 71), 0)
    present = draw_present(jax.random.fold_in(splits[4], 71), 0)
    return dict(margin=margin, fock_matrix=fock_matrix, density=density, present=present)


step_scale = 0.015625


def padded_rows(matrix, reach_rows):
    return jnp.pad(matrix, ((reach_rows, reach_rows), (0, 0), (0, 0)))


def band_product(left_band, right_wide, present):
    row_count = left_band.shape[0]
    block_size = left_band.shape[1]
    band_count = present.shape[1]
    half_band = (band_count - 1) // 2
    left_blocks = left_band.astype(jnp.float32).reshape(row_count, block_size, band_count, block_size)
    right_blocks = right_wide.astype(jnp.float32).reshape(right_wide.shape[0], block_size, band_count, block_size)
    accumulated = jnp.zeros((row_count, block_size, band_count, block_size), jnp.float32)
    for p in range(band_count):
        first_col = max(0, half_band - p)
        last_col = min(band_count, band_count + half_band - p)
        contribution = jnp.einsum("rik,rkqc->riqc", left_blocks[:, :, p, :], right_blocks[p:p + row_count, :, first_col:last_col, :], precision=lax.Precision.HIGHEST)
        accumulated = accumulated + jnp.pad(contribution, ((0, 0), (0, 0), (first_col + p - half_band, band_count - (last_col + p - half_band)), (0, 0)))
    keep_mask = present.astype(jnp.float32)[:, None, :, None]
    return (accumulated * keep_mask).reshape(row_count, block_size, band_count * block_size)


def band_mirror(wide, band_count):
    half_band = (band_count - 1) // 2
    block_size = wide.shape[1]
    row_count = wide.shape[0] - 2 * half_band
    wide_blocks = wide.reshape(wide.shape[0], block_size, band_count, block_size)
    slot_list = [jnp.swapaxes(wide_blocks[s:s + row_count, :, band_count - 1 - s, :], 1, 2) for s in range(band_count)]
    return jnp.stack(slot_list, axis=2).reshape(row_count, block_size, band_count * block_size)


def reference(margin, fock_matrix, density, present):
    band_count = present.shape[1]
    half_band = (band_count - 1) // 2
    margin_wide = padded_rows(margin, half_band)
    dens_over = band_product(density, margin_wide, present).astype(jnp.bfloat16)
    fock_dens = band_product(fock_matrix, padded_rows(dens_over, half_band), present).astype(jnp.bfloat16)
    gradient = fock_dens.astype(jnp.float32) - band_mirror(padded_rows(fock_dens, half_band), band_count).astype(jnp.float32)
    step_matrix = (-step_scale * gradient).astype(jnp.bfloat16)
    step_wide = padded_rows(step_matrix, half_band)
    first_term = band_product(dens_over, step_wide, present).astype(jnp.bfloat16)
    commuted = first_term.astype(jnp.float32) + band_mirror(padded_rows(first_term, half_band), band_count).astype(jnp.float32)
    commuted_half = commuted.astype(jnp.bfloat16)
    comm_over = band_product(commuted_half, margin_wide, present).astype(jnp.bfloat16)
    second_term = band_product(comm_over, step_wide, present).astype(jnp.bfloat16)
    second_mirror = band_mirror(padded_rows(second_term, half_band), band_count).astype(jnp.float32)
    updated = density.astype(jnp.float32) + commuted + 0.5 * (second_term.astype(jnp.float32) + second_mirror)
    return gradient, updated
```

```python
import functools

import jax
import jax.numpy as jnp
from jax import lax
from jax.experimental import pallas as pl
from jax.experimental.pallas import tpu as pltpu
from jax.sharding import PartitionSpec as P

STEP_SCALE = 0.015625
SYMMETRIC = False


def kernel(ncol, n, b, half, sym, margin, fock, density, present, grad, upd,
           sw, xw, tw, xrow, trow, dv, fv, mv, gd, gm, cf, ch, co, qd, qm,
           lsem, wsend, wrecv, msend, mrecv):
    band = 2 * half + 1
    r = lax.axis_index("row") * ncol + lax.axis_index("col")
    k = r // 2
    core = r % 2
    chips = n // 2

    def device(t):
        return {"row": t // ncol, "col": t % ncol}

    def col(i, count=1):
        return pl.ds(pl.multiple_of(i * b, b), count * b)

    def valid_chip(e):
        return jnp.logical_and(k + e >= 0, k + e < chips)

    def valid(d):
        return jnp.logical_and(r + d >= 0, r + d < n)

    sibling = device(r + 1 - 2 * core)
    offsets = [d for d in range(-half, half + 1) if d != 0]
    reach = half // 2
    hops = [e for m in range(1, reach + 1) for e in (m, -m)]

    loads = [
        pltpu.make_async_copy(margin.at[0], mv, lsem.at[0]),
        pltpu.make_async_copy(density.at[0], dv, lsem.at[1]),
        pltpu.make_async_copy(fock.at[0], fv, lsem.at[2]),
    ]
    for c in loads:
        c.start()

    barrier = pltpu.get_barrier_semaphore()
    for d in offsets:
        @pl.when(valid(d))
        def _():
            pl.semaphore_signal(barrier, inc=1, device_id=device(r + d),
                                device_id_type=pl.DeviceIdType.MESH)

    for e in hops:
        @pl.when(jnp.logical_not(valid_chip(e)))
        def _():
            p = half + 2 * e
            for w in (sw, xw, tw):
                w[p * b:(p + 2) * b, :] = jnp.zeros((2 * b, w.shape[1]), w.dtype)
    for d in offsets:
        @pl.when(jnp.logical_not(valid(-d)))
        def _():
            for m in (gm.at[0], gm.at[1], gm.at[2]):
                m[half - d] = jnp.zeros((b, b), gm.dtype)

    expected = jnp.minimum(r, half) + jnp.minimum(n - 1 - r, half)
    pl.semaphore_wait(barrier, expected)

    pending = []

    def window_plan(symmetric):
        plan = []
        for e in hops:
            if e > 0:
                s0 = 2 * e - 1
                plan.append((e, s0, band - s0, core - 1))
            else:
                plan.append((e, 0, band + 2 * e + 1, core - 2 * e))
        return plan

    def spread(phase, own, w, symmetric):
        plan = window_plan(symmetric)
        here = pl.ds(pl.multiple_of((half + core) * b, b), b)
        copies = []
        for i, (e, s0, count, c0) in enumerate(plan):
            p = half - 2 * e + core
            spot = w.at[pl.ds(pl.multiple_of(p * b, b), b), col(c0 + 1, count)]
            src = own.at[:, s0 * b:(s0 + count) * b]
            send = pltpu.make_async_remote_copy(
                src_ref=src, dst_ref=spot, send_sem=wsend.at[phase, i],
                recv_sem=wrecv.at[phase, i], device_id=device(r + 2 * e),
                device_id_type=pl.DeviceIdType.MESH)
            relay = pltpu.make_async_remote_copy(
                src_ref=spot, dst_ref=spot, send_sem=wsend.at[phase, 6 + i],
                recv_sem=wrecv.at[phase, 6 + i], device_id=sibling,
                device_id_type=pl.DeviceIdType.MESH)

            @pl.when(valid_chip(e))
            def _():
                send.start()
            copies.append((e, send, relay))
        share = pltpu.make_async_remote_copy(
            src_ref=own, dst_ref=w.at[here, col(core + 1, band)],
            send_sem=wsend.at[phase, 12], recv_sem=wrecv.at[phase, 12],
            device_id=sibling, device_id_type=pl.DeviceIdType.MESH)
        share.start()
        w[here, col(core + 1, band)] = own[...]
        for e, send, relay in copies:
            @pl.when(valid_chip(-e))
            def _():
                send.wait_recv()
                relay.start()
        share.wait_recv()
        for e, send, relay in copies:
            @pl.when(valid_chip(-e))
            def _():
                relay.wait_recv()
            pending.append((valid_chip(e), send))
            pending.append((valid_chip(-e), relay))
        pending.append((None, share))

    def mirror(phase, own, m):
        copies = []
        for i, d in enumerate(sorted(offsets, key=lambda v: -abs(v))):
            c = pltpu.make_async_remote_copy(
                src_ref=own.at[:, (half + d) * b:(half + d + 1) * b],
                dst_ref=m.at[half - d], send_sem=msend.at[phase, i],
                recv_sem=mrecv.at[phase, i], device_id=device(r + d),
                device_id_type=pl.DeviceIdType.MESH)

            @pl.when(valid(d))
            def _():
                c.start()
            copies.append((d, c))
        m[half] = own[:, half * b:(half + 1) * b]
        for d, c in copies:
            @pl.when(valid(-d))
            def _():
                c.wait_recv()
            pending.append((valid(d), c))

    def product(left, w, out):
        for c in range(band):
            lo, hi = max(0, c - half), min(band, c + half + 1)
            rhs = w[pl.ds(pl.multiple_of((core + lo) * b, b), (hi - lo) * b), col(core + 1 + c)]
            acc = jnp.dot(left[:, lo * b:hi * b], rhs, preferred_element_type=jnp.float32)
            keep = present[0, c].astype(jnp.float32)
            out[:, c * b:(c + 1) * b] = (acc * keep).astype(out.dtype)

    loads[0].wait()
    spread(0, mv, sw, sym)
    loads[1].wait()
    product(dv, sw, xrow)
    spread(1, xrow, xw, False)
    loads[2].wait()
    product(fv, xw, gd)
    mirror(0, gd, gm.at[0])
    for c in range(band):
        cols = slice(c * b, (c + 1) * b)
        g = gd[:, cols].astype(jnp.float32) - gm[0, c].T.astype(jnp.float32)
        grad[0, :, cols] = g
        trow[:, cols] = (-STEP_SCALE * g).astype(trow.dtype)
    spread(2, trow, tw, sym)
    product(xrow, tw, cf)
    mirror(1, cf, gm.at[1])
    for c in range(band):
        cols = slice(c * b, (c + 1) * b)
        v = cf[:, cols].astype(jnp.float32) + gm[1, c].T.astype(jnp.float32)
        upd[0, :, cols] = dv[:, cols].astype(jnp.float32) + v
        ch[:, cols] = v.astype(ch.dtype)
    product(ch, sw, co)
    product(co, tw, qd)
    mirror(2, qd, gm.at[2])
    for c in range(band):
        cols = slice(c * b, (c + 1) * b)
        q = qd[:, cols].astype(jnp.float32) + gm[2, c].T.astype(jnp.float32)
        upd[0, :, cols] += 0.5 * q
    for cond, c in pending:
        if cond is None:
            c.wait_send()
        else:
            @pl.when(cond)
            def _():
                c.wait_send()


def local(ncol, n, margin, fock_matrix, density, present):
    rows, b, width = margin.shape
    band = present.shape[1]
    half = (band - 1) // 2
    bf = jnp.bfloat16
    row = pltpu.VMEM((b, width), bf)
    wide = pltpu.VMEM(((band + 1) * b, (band + 3) * b), bf)
    out = jax.ShapeDtypeStruct((rows, b, width), jnp.float32)
    return pl.pallas_call(
        functools.partial(kernel, ncol, n, b, half, SYMMETRIC),
        out_shape=(out, out),
        in_specs=[pl.BlockSpec(memory_space=pl.ANY)] * 3
        + [pl.BlockSpec(memory_space=pltpu.SMEM)],
        out_specs=[pl.BlockSpec(memory_space=pltpu.VMEM)] * 2,
        scratch_shapes=[
            wide, wide, wide, row, row, row, row, row,
            row, pltpu.VMEM((3, band, b, b), bf), row, row, row, row,
            pltpu.VMEM((8, 128), bf),
            pltpu.SemaphoreType.DMA((3,)),
            pltpu.SemaphoreType.DMA((3, 13)),
            pltpu.SemaphoreType.DMA((3, 13)),
            pltpu.SemaphoreType.DMA((3, 2 * half)),
            pltpu.SemaphoreType.DMA((3, 2 * half)),
        ],
        compiler_params=pltpu.CompilerParams(
            collective_id=0, has_side_effects=True, vmem_limit_bytes=48 * 1024 * 1024),
        name="density_step",
    )(margin, fock_matrix, density, present)


def solution(mesh):
    nrow, ncol = mesh.shape["row"], mesh.shape["col"]
    spec3 = P(("row", "col"), None, None)
    return jax.shard_map(
        functools.partial(local, ncol, nrow * ncol), mesh=mesh,
        in_specs=(spec3, spec3, spec3, P(("row", "col"), None)),
        out_specs=(spec3, spec3), check_vma=False)
```

```python
import functools

import jax
import jax.numpy as jnp
from jax import lax
from jax.experimental import pallas as pl
from jax.experimental.pallas import tpu as pltpu
from jax.sharding import PartitionSpec as P

STEP_SCALE = 0.015625


def kernel(ncol, n, b, half, margin, fock, density, kept, grad, upd,
           sw, xw, tw, xrow, trow, dv, fv, mv, gd, gm, cf, cm, ch, co, qd, present,
           lsem, wsend, wrecv, msend, mrecv):
    band = 2 * half + 1
    r = lax.axis_index("row") * ncol + lax.axis_index("col")
    k = r // 2
    core = r % 2
    chips = n // 2

    def device(t):
        return {"row": t // ncol, "col": t % ncol}

    def col(i, count=1):
        return pl.ds(pl.multiple_of(i * b, b), count * b)

    def valid_chip(e):
        return jnp.logical_and(k + e >= 0, k + e < chips)

    def valid(d):
        return jnp.logical_and(r + d >= 0, r + d < n)

    sibling = device(r + 1 - 2 * core)
    offsets = [d for d in range(-half, half + 1) if d != 0]
    reach = half // 2
    hops = [e for m in range(1, reach + 1) for e in (m, -m)]

    loads = [
        pltpu.make_async_copy(margin.at[0], mv, lsem.at[0]),
        pltpu.make_async_copy(density.at[0], dv, lsem.at[1]),
        pltpu.make_async_copy(fock.at[0], fv, lsem.at[2]),
        pltpu.make_async_copy(kept, present, lsem.at[3]),
    ]
    for c in loads:
        c.start()

    barrier = pltpu.get_barrier_semaphore()
    for d in offsets:
        @pl.when(valid(d))
        def _():
            pl.semaphore_signal(barrier, inc=1, device_id=device(r + d),
                                device_id_type=pl.DeviceIdType.MESH)

    for e in hops:
        @pl.when(jnp.logical_not(valid_chip(e)))
        def _():
            p = half + 2 * e
            for w in (sw, xw, tw):
                w[p * b:(p + 2) * b, :] = jnp.zeros((2 * b, w.shape[1]), w.dtype)
    for d in offsets:
        @pl.when(jnp.logical_not(valid(-d)))
        def _():
            for m in (gm.at[0], gm.at[1]):
                m[half - d] = jnp.zeros((b, b), gm.dtype)

    expected = jnp.minimum(r, half) + jnp.minimum(n - 1 - r, half)
    pl.semaphore_wait(barrier, expected)

    pending = []

    def window_plan(symmetric):
        plan = []
        for e in hops:
            m = abs(e)
            if symmetric:
                near = half - 2 * m + 2
                if e > 0:
                    plan.append((e, 2 * m - core, near, 0))
                    if 4 * m - 1 <= half:
                        plan.append((e, band - 2, 2, half + 1 + core))
                else:
                    plan.append((e, half - core, near, half + 2 * m))
            elif e > 0:
                plan.append((e, 2 * m - 1, band - 2 * m + 1, core - 1))
            else:
                plan.append((e, 0, band - 2 * m + 1, core + 2 * m))
        return plan

    def known_blocks():
        known = set()
        for m in range(1, reach + 1):
            for c in (0, 1):
                known |= {(half - 2 * m + c, j) for j in range(half - 2 * m + 2)}
                known |= {(half + 2 * m + c, j) for j in range(half + 2 * m, band + 1)}
                if 4 * m - 1 <= half:
                    known |= {(half - 2 * m + c, half + 1 + c + j) for j in (0, 1)}
        return known

    def reflect(w, sign, own_rows):
        known = known_blocks()
        middle = (half, half + 1)
        for i in range(band + 1):
            for j in range(band + 1):
                if abs(i - j) > half or i in middle or (i, j) in known:
                    continue
                if (j in middle) != own_rows:
                    continue
                block = w[j * b:(j + 1) * b, (i + 1) * b:(i + 2) * b].T
                w[i * b:(i + 1) * b, (j + 1) * b:(j + 2) * b] = block if sign > 0 else -block

    def spread(phase, own, w, sign, beside=None):
        plan = window_plan(sign != 0)
        here = pl.ds(pl.multiple_of((half + core) * b, b), b)
        copies = []
        for i, (e, s0, count, c0) in enumerate(plan):
            p = half - 2 * e + core
            spot = w.at[pl.ds(pl.multiple_of(p * b, b), b), col(c0 + 1, count)]
            send = pltpu.make_async_remote_copy(
                src_ref=own.at[:, col(s0, count)], dst_ref=spot,
                send_sem=wsend.at[phase, i], recv_sem=wrecv.at[phase, i],
                device_id=device(r + 2 * e), device_id_type=pl.DeviceIdType.MESH)
            relay = pltpu.make_async_remote_copy(
                src_ref=spot, dst_ref=spot, send_sem=wsend.at[phase, 6 + i],
                recv_sem=wrecv.at[phase, 6 + i], device_id=sibling,
                device_id_type=pl.DeviceIdType.MESH)

            @pl.when(valid_chip(e))
            def _():
                send.start()
            copies.append((e, send, relay))
        share = pltpu.make_async_remote_copy(
            src_ref=own, dst_ref=w.at[here, col(core + 1, band)],
            send_sem=wsend.at[phase, 12], recv_sem=wrecv.at[phase, 12],
            device_id=sibling, device_id_type=pl.DeviceIdType.MESH)
        share.start()
        w[here, col(core + 1, band)] = own[...]
        if sign:
            share.wait_recv()
            reflect(w, sign, True)
        if beside is not None:
            beside()
        for e, send, relay in copies:
            @pl.when(valid_chip(-e))
            def _():
                send.wait_recv()
                relay.start()
        if not sign:
            share.wait_recv()
        for e, send, relay in copies:
            @pl.when(valid_chip(-e))
            def _():
                relay.wait_recv()
            pending.append((valid_chip(e), send))
            pending.append((valid_chip(-e), relay))
        pending.append((None, share))
        if sign:
            reflect(w, sign, False)

    def mirror(phase, own, m):
        copies = []
        for i, d in enumerate(sorted(offsets, key=lambda v: -abs(v))):
            c = pltpu.make_async_remote_copy(
                src_ref=own.at[:, (half + d) * b:(half + d + 1) * b],
                dst_ref=m.at[half - d], send_sem=msend.at[phase, i],
                recv_sem=mrecv.at[phase, i], device_id=device(r + d),
                device_id_type=pl.DeviceIdType.MESH)

            @pl.when(valid(d))
            def _():
                c.start()
            copies.append((d, c))
        m[half] = own[:, half * b:(half + 1) * b]
        for d, c in copies:
            @pl.when(valid(-d))
            def _():
                c.wait_recv()
            pending.append((valid(d), c))

    def product(left, w, out):
        for c in range(band):
            lo, hi = max(0, c - half), min(band, c + half + 1)
            rhs = w[pl.ds(pl.multiple_of((core + lo) * b, b), (hi - lo) * b), col(core + 1 + c)]
            acc = jnp.dot(left[:, lo * b:hi * b], rhs, preferred_element_type=jnp.float32)
            keep = present[0, c].astype(jnp.float32)
            out[:, c * b:(c + 1) * b] = (acc * keep).astype(out.dtype)

    def transposed_first():
        for c in range(band):
            lo, hi = max(0, c - half), min(band, c + half + 1)
            rhs = xw[pl.ds(pl.multiple_of((core + c) * b, b), b), col(core + 1 + lo, hi - lo)]
            acc = lax.dot_general(trow[:, lo * b:hi * b], rhs, (((1,), (1,)), ((), ())),
                                  preferred_element_type=jnp.float32)
            keep = present[0, c].astype(jnp.float32)
            cm[:, c * b:(c + 1) * b] = (acc * -keep).astype(cm.dtype)

    loads[0].wait()
    spread(0, mv, sw, 1)
    loads[1].wait()
    loads[3].wait()
    product(dv, sw, xrow)
    spread(1, xrow, xw, 0)
    loads[2].wait()
    product(fv, xw, gd)
    mirror(0, gd, gm.at[0])
    for c in range(band):
        cols = slice(c * b, (c + 1) * b)
        g = gd[:, cols].astype(jnp.float32) - gm[0, c].T.astype(jnp.float32)
        grad[0, :, cols] = g
        trow[:, cols] = (-STEP_SCALE * g).astype(trow.dtype)
    spread(2, trow, tw, -1, transposed_first)
    product(xrow, tw, cf)
    v = cf[...].astype(jnp.float32) + cm[...].astype(jnp.float32)
    upd[0] = dv[...].astype(jnp.float32) + v
    ch[...] = v.astype(ch.dtype)
    product(ch, sw, co)
    product(co, tw, qd)
    mirror(1, qd, gm.at[1])
    for c in range(band):
        cols = slice(c * b, (c + 1) * b)
        q = qd[:, cols].astype(jnp.float32) + gm[1, c].T.astype(jnp.float32)
        upd[0, :, cols] += 0.5 * q
    for cond, c in pending:
        if cond is None:
            c.wait_send()
        else:
            @pl.when(cond)
            def _():
                c.wait_send()


def local(ncol, n, margin, fock_matrix, density, present):
    rows, b, width = margin.shape
    band = present.shape[1]
    half = (band - 1) // 2
    bf = jnp.bfloat16
    row = pltpu.VMEM((b, width), bf)
    wide = pltpu.VMEM(((band + 1) * b, (band + 3) * b), bf)
    out = jax.ShapeDtypeStruct((rows, b, width), jnp.float32)
    return pl.pallas_call(
        functools.partial(kernel, ncol, n, b, half),
        out_shape=(out, out),
        in_specs=[pl.BlockSpec(memory_space=pl.ANY)] * 4,
        out_specs=[pl.BlockSpec(memory_space=pltpu.VMEM)] * 2,
        scratch_shapes=[
            wide, wide, wide, row, row, row, row, row,
            row, pltpu.VMEM((2, band, b, b), bf), row, row, row, row, row,
            pltpu.SMEM((rows, band), jnp.int32),
            pltpu.SemaphoreType.DMA((4,)),
            pltpu.SemaphoreType.DMA((3, 13)),
            pltpu.SemaphoreType.DMA((3, 13)),
            pltpu.SemaphoreType.DMA((2, 2 * half)),
            pltpu.SemaphoreType.DMA((2, 2 * half)),
        ],
        compiler_params=pltpu.CompilerParams(
            collective_id=0, has_side_effects=True, vmem_limit_bytes=67043328),
        name="density_step",
    )(margin, fock_matrix, density, present)


def solution(mesh):
    nrow, ncol = mesh.shape["row"], mesh.shape["col"]
    spec3 = P(("row", "col"), None, None)
    return jax.shard_map(
        functools.partial(local, ncol, nrow * ncol), mesh=mesh,
        in_specs=(spec3, spec3, spec3, P(("row", "col"), None)),
        out_specs=(spec3, spec3), check_vma=False)
```

```python
import functools

import jax
import jax.numpy as jnp
from jax import lax
from jax.experimental import pallas as pl
from jax.experimental.pallas import tpu as pltpu
from jax.sharding import PartitionSpec as P

STEP_SCALE = 0.015625


def kernel(ncol, n, b, half, margin, fock, density, kept, grad, upd,
           sw, xw, tw, xrow, trow, dv, fv, mv, gd, gm, cf, cm, ch, co, qd, present,
           lsem, wsend, wrecv, msend, mrecv):
    band = 2 * half + 1
    r = lax.axis_index("row") * ncol + lax.axis_index("col")
    k = r // 2
    core = r % 2
    chips = n // 2

    def device(t):
        return {"row": t // ncol, "col": t % ncol}

    def col(i, count=1):
        return pl.ds(pl.multiple_of(i * b, b), count * b)

    def valid_chip(e):
        return jnp.logical_and(k + e >= 0, k + e < chips)

    def valid(d):
        return jnp.logical_and(r + d >= 0, r + d < n)

    sibling = device(r + 1 - 2 * core)
    offsets = [d for d in range(-half, half + 1) if d != 0]
    reach = half // 2
    hops = [e for m in range(1, reach + 1) for e in (m, -m)]

    loads = [
        pltpu.make_async_copy(margin.at[0], mv, lsem.at[0]),
        pltpu.make_async_copy(density.at[0], dv, lsem.at[1]),
        pltpu.make_async_copy(fock.at[0], fv, lsem.at[2]),
        pltpu.make_async_copy(kept, present, lsem.at[3]),
    ]
    for c in loads:
        c.start()

    barrier = pltpu.get_barrier_semaphore()
    for d in offsets:
        @pl.when(valid(d))
        def _():
            pl.semaphore_signal(barrier, inc=1, device_id=device(r + d),
                                device_id_type=pl.DeviceIdType.MESH)

    for e in hops:
        @pl.when(jnp.logical_not(valid_chip(e)))
        def _():
            p = half + 2 * e
            for w in (sw, xw, tw):
                w[p * b:(p + 2) * b, :] = jnp.zeros((2 * b, w.shape[1]), w.dtype)
    for d in offsets:
        @pl.when(jnp.logical_not(valid(-d)))
        def _():
            for m in (gm.at[0], gm.at[1]):
                m[half - d] = jnp.zeros((b, b), gm.dtype)

    expected = jnp.minimum(r, half) + jnp.minimum(n - 1 - r, half)
    pl.semaphore_wait(barrier, expected)

    pending = []

    def window_plan(symmetric, c):
        plan = []
        for e in hops:
            m = abs(e)
            p = half - 2 * e + c
            if not symmetric:
                lo, hi = max(0, p - half), min(band, p + half)
                plan.append((e, p, lo, hi - lo + 1))
            elif e > 0:
                plan.append((e, p, 0, p + 1))
                if m == 1 and c == 1:
                    plan.append((e, p, half + 2, 2))
            else:
                plan.append((e, p, p, band + 1 - p))
                if m == 1 and c == 0:
                    plan.append((e, p, half - 2, 1))
        return plan

    def known_blocks():
        return {(p, j) for c in (0, 1) for _, p, lo, count in window_plan(True, c)
                for j in range(lo, lo + count)}

    def reflect(w, sign, own_rows):
        known = known_blocks()
        middle = (half, half + 1)
        for i in range(band + 1):
            for j in range(band + 1):
                if abs(i - j) > half or i in middle or (i, j) in known:
                    continue
                if (j in middle) != own_rows:
                    continue
                block = w[j * b:(j + 1) * b, (i + 1) * b:(i + 2) * b].T
                w[i * b:(i + 1) * b, (j + 1) * b:(j + 2) * b] = block if sign > 0 else -block

    def both(x, y):
        return jnp.logical_and(x, y)

    def spread(phase, own, w, sign, beside=None):
        here = pl.ds(pl.multiple_of((half + core) * b, b), b)
        sends, relays = [], []
        for cc in (0, 1):
            mine, theirs = core == cc, core == 1 - cc
            for i, (e, p, lo, count) in enumerate(window_plan(sign != 0, cc)):
                spot = w.at[p * b:(p + 1) * b, (lo + 1) * b:(lo + 1 + count) * b]
                s0 = lo - p + half
                send = pltpu.make_async_remote_copy(
                    src_ref=own.at[:, s0 * b:(s0 + count) * b], dst_ref=spot,
                    send_sem=wsend.at[phase, i], recv_sem=wrecv.at[phase, i],
                    device_id=device(r + 2 * e), device_id_type=pl.DeviceIdType.MESH)
                out, back = both(mine, valid_chip(e)), both(mine, valid_chip(-e))
                relay = None
                if 0 < p < band:
                    relay = pltpu.make_async_remote_copy(
                        src_ref=spot, dst_ref=spot, send_sem=wsend.at[phase, 6 + i],
                        recv_sem=wrecv.at[phase, 6 + i], device_id=sibling,
                        device_id_type=pl.DeviceIdType.MESH)
                    relays.append((relay, back, both(theirs, valid_chip(-e))))

                @pl.when(out)
                def _():
                    send.start()
                sends.append((send, relay, out, back))
        share = pltpu.make_async_remote_copy(
            src_ref=own, dst_ref=w.at[here, col(core + 1, band)],
            send_sem=wsend.at[phase, 12], recv_sem=wrecv.at[phase, 12],
            device_id=sibling, device_id_type=pl.DeviceIdType.MESH)
        share.start()
        w[here, col(core + 1, band)] = own[...]
        if sign:
            share.wait_recv()
            reflect(w, sign, True)
        if beside is not None:
            beside()
        for send, relay, out, back in sends:
            @pl.when(back)
            def _():
                send.wait_recv()
                if relay is not None:
                    relay.start()
            pending.append((out, send))
        if not sign:
            share.wait_recv()
        for relay, started, arriving in relays:
            @pl.when(arriving)
            def _():
                relay.wait_recv()
            pending.append((started, relay))
        pending.append((None, share))
        if sign:
            reflect(w, sign, False)

    def mirror(phase, own, m):
        copies = []
        for i, d in enumerate(sorted(offsets, key=lambda v: -abs(v))):
            c = pltpu.make_async_remote_copy(
                src_ref=own.at[:, (half + d) * b:(half + d + 1) * b],
                dst_ref=m.at[half - d], send_sem=msend.at[phase, i],
                recv_sem=mrecv.at[phase, i], device_id=device(r + d),
                device_id_type=pl.DeviceIdType.MESH)

            @pl.when(valid(d))
            def _():
                c.start()
            copies.append((d, c))
        m[half] = own[:, half * b:(half + 1) * b]
        for d, c in copies:
            @pl.when(valid(-d))
            def _():
                c.wait_recv()
            pending.append((valid(d), c))

    def product(left, w, out):
        for c in range(band):
            lo, hi = max(0, c - half), min(band, c + half + 1)
            rhs = w[pl.ds(pl.multiple_of((core + lo) * b, b), (hi - lo) * b), col(core + 1 + c)]
            acc = jnp.dot(left[:, lo * b:hi * b], rhs, preferred_element_type=jnp.float32)
            keep = present[0, c].astype(jnp.float32)
            out[:, c * b:(c + 1) * b] = (acc * keep).astype(out.dtype)

    def transposed_first():
        for c in range(band):
            lo, hi = max(0, c - half), min(band, c + half + 1)
            rhs = xw[pl.ds(pl.multiple_of((core + c) * b, b), b), col(core + 1 + lo, hi - lo)]
            acc = lax.dot_general(trow[:, lo * b:hi * b], rhs, (((1,), (1,)), ((), ())),
                                  preferred_element_type=jnp.float32)
            keep = present[0, c].astype(jnp.float32)
            cm[:, c * b:(c + 1) * b] = (acc * -keep).astype(cm.dtype)

    loads[0].wait()
    spread(0, mv, sw, 1)
    loads[1].wait()
    loads[3].wait()
    product(dv, sw, xrow)
    spread(1, xrow, xw, 0)
    loads[2].wait()
    product(fv, xw, gd)
    mirror(0, gd, gm.at[0])
    for c in range(band):
        cols = slice(c * b, (c + 1) * b)
        g = gd[:, cols].astype(jnp.float32) - gm[0, c].T.astype(jnp.float32)
        grad[0, :, cols] = g
        trow[:, cols] = (-STEP_SCALE * g).astype(trow.dtype)
    spread(2, trow, tw, -1, transposed_first)
    product(xrow, tw, cf)
    v = cf[...].astype(jnp.float32) + cm[...].astype(jnp.float32)
    upd[0] = dv[...].astype(jnp.float32) + v
    ch[...] = v.astype(ch.dtype)
    product(ch, sw, co)
    product(co, tw, qd)
    mirror(1, qd, gm.at[1])
    for c in range(band):
        cols = slice(c * b, (c + 1) * b)
        q = qd[:, cols].astype(jnp.float32) + gm[1, c].T.astype(jnp.float32)
        upd[0, :, cols] += 0.5 * q
    for cond, c in pending:
        if cond is None:
            c.wait_send()
        else:
            @pl.when(cond)
            def _():
                c.wait_send()


def local(ncol, n, margin, fock_matrix, density, present):
    rows, b, width = margin.shape
    band = present.shape[1]
    half = (band - 1) // 2
    bf = jnp.bfloat16
    row = pltpu.VMEM((b, width), bf)
    wide = pltpu.VMEM(((band + 1) * b, (band + 3) * b), bf)
    out = jax.ShapeDtypeStruct((rows, b, width), jnp.float32)
    return pl.pallas_call(
        functools.partial(kernel, ncol, n, b, half),
        out_shape=(out, out),
        in_specs=[pl.BlockSpec(memory_space=pltpu.HBM)] * 4,
        out_specs=[pl.BlockSpec(memory_space=pltpu.VMEM)] * 2,
        scratch_shapes=[
            wide, wide, wide, row, row, row, row, row,
            row, pltpu.VMEM((2, band, b, b), bf), row, row, row, row, row,
            pltpu.SMEM((rows, band), jnp.int32),
            pltpu.SemaphoreType.DMA((4,)),
            pltpu.SemaphoreType.DMA((3, 13)),
            pltpu.SemaphoreType.DMA((3, 13)),
            pltpu.SemaphoreType.DMA((2, 2 * half)),
            pltpu.SemaphoreType.DMA((2, 2 * half)),
        ],
        compiler_params=pltpu.CompilerParams(
            collective_id=0, has_side_effects=True, vmem_limit_bytes=48 * 1024 * 1024),
        name="density_step",
    )(margin, fock_matrix, density, present)


def solution(mesh):
    nrow, ncol = mesh.shape["row"], mesh.shape["col"]
    spec3 = P(("row", "col"), None, None)
    return jax.shard_map(
        functools.partial(local, ncol, nrow * ncol), mesh=mesh,
        in_specs=(spec3, spec3, spec3, P(("row", "col"), None)),
        out_specs=(spec3, spec3), check_vma=False)
```

```python
import functools

import jax
import jax.numpy as jnp
from jax import lax
from jax.experimental import pallas as pl
from jax.experimental.pallas import tpu as pltpu
from jax.sharding import PartitionSpec as P

STEP_SCALE = 0.015625


def kernel(ncol, n, b, half, margin, fock, density, kept, *rest):
    outs, rest = rest[:6], rest[6:]
    (sw, xw, tw, xrow, trow, dv, fv, mv, gd, gt, gm, cf, cm, ch, co, qd, qt, present,
     lsem, osem, wsend, wrecv, msend, mrecv) = rest
    band = 2 * half + 1
    r = lax.axis_index("row") * ncol + lax.axis_index("col")
    k = r // 2
    core = r % 2
    chips = n // 2

    def device(t):
        return {"row": t // ncol, "col": t % ncol}

    def col(i, count=1):
        return pl.ds(pl.multiple_of(i * b, b), count * b)

    def valid_chip(e):
        return jnp.logical_and(k + e >= 0, k + e < chips)

    def valid(d):
        return jnp.logical_and(r + d >= 0, r + d < n)

    sibling = device(r + 1 - 2 * core)
    offsets = [d for d in range(-half, half + 1) if d != 0]
    reach = half // 2
    hops = [e for m in range(1, reach + 1) for e in (m, -m)]

    loads = [
        pltpu.make_async_copy(margin.at[0], mv, lsem.at[0]),
        pltpu.make_async_copy(density.at[0], dv, lsem.at[1]),
        pltpu.make_async_copy(fock.at[0], fv, lsem.at[2]),
        pltpu.make_async_copy(kept, present, lsem.at[3]),
    ]
    for c in loads:
        c.start()

    barrier = pltpu.get_barrier_semaphore()
    for d in offsets:
        @pl.when(valid(d))
        def _():
            pl.semaphore_signal(barrier, inc=1, device_id=device(r + d),
                                device_id_type=pl.DeviceIdType.MESH)

    for e in hops:
        @pl.when(jnp.logical_not(valid_chip(e)))
        def _():
            p = half + 2 * e
            for w in (sw, xw, tw):
                w[p * b:(p + 2) * b, :] = jnp.zeros((2 * b, w.shape[1]), w.dtype)
    for d in offsets:
        @pl.when(jnp.logical_not(valid(-d)))
        def _():
            for m in (gm.at[0], gm.at[1]):
                m[half - d] = jnp.zeros((b, b), gm.dtype)

    expected = jnp.minimum(r, half) + jnp.minimum(n - 1 - r, half)
    pl.semaphore_wait(barrier, expected)

    pending = []

    def window_plan(symmetric, c):
        plan = []
        for e in hops:
            m = abs(e)
            p = half - 2 * e + c
            if not symmetric:
                lo, hi = max(0, p - half), min(band, p + half)
                plan.append((e, p, lo, hi - lo + 1))
            elif e > 0:
                plan.append((e, p, 0, p + 1))
                if m == 1 and c == 1:
                    plan.append((e, p, half + 2, 2))
            else:
                plan.append((e, p, p, band + 1 - p))
                if m == 1 and c == 0:
                    plan.append((e, p, half - 2, 1))
        return plan

    def known_blocks():
        return {(p, j) for c in (0, 1) for _, p, lo, count in window_plan(True, c)
                for j in range(lo, lo + count)}

    def reflect(w, sign, own_rows):
        known = known_blocks()
        middle = (half, half + 1)
        for i in range(band + 1):
            for j in range(band + 1):
                if abs(i - j) > half or i in middle or (i, j) in known:
                    continue
                if (j in middle) != own_rows:
                    continue
                block = w[j * b:(j + 1) * b, (i + 1) * b:(i + 2) * b].T
                w[i * b:(i + 1) * b, (j + 1) * b:(j + 2) * b] = block if sign > 0 else -block

    def both(x, y):
        return jnp.logical_and(x, y)

    def spread(phase, own, w, sign, beside=None):
        here = pl.ds(pl.multiple_of((half + core) * b, b), b)
        sends, relays = [], []
        for cc in (0, 1):
            mine, theirs = core == cc, core == 1 - cc
            for i, (e, p, lo, count) in enumerate(window_plan(sign != 0, cc)):
                spot = w.at[p * b:(p + 1) * b, (lo + 1) * b:(lo + 1 + count) * b]
                s0 = lo - p + half
                send = pltpu.make_async_remote_copy(
                    src_ref=own.at[:, s0 * b:(s0 + count) * b], dst_ref=spot,
                    send_sem=wsend.at[phase, i], recv_sem=wrecv.at[phase, i],
                    device_id=device(r + 2 * e), device_id_type=pl.DeviceIdType.MESH)
                out, back = both(mine, valid_chip(e)), both(mine, valid_chip(-e))
                relay = None
                if 0 < p < band:
                    relay = pltpu.make_async_remote_copy(
                        src_ref=spot, dst_ref=spot, send_sem=wsend.at[phase, 6 + i],
                        recv_sem=wrecv.at[phase, 6 + i], device_id=sibling,
                        device_id_type=pl.DeviceIdType.MESH)
                    relays.append((relay, back, both(theirs, valid_chip(-e))))

                @pl.when(out)
                def _():
                    send.start()
                sends.append((send, relay, out, back))
        share = pltpu.make_async_remote_copy(
            src_ref=own, dst_ref=w.at[here, col(core + 1, band)],
            send_sem=wsend.at[phase, 12], recv_sem=wrecv.at[phase, 12],
            device_id=sibling, device_id_type=pl.DeviceIdType.MESH)
        share.start()
        w[here, col(core + 1, band)] = own[...]
        if sign:
            share.wait_recv()
            reflect(w, sign, True)
        if beside is not None:
            beside()
        for send, relay, out, back in sends:
            @pl.when(back)
            def _():
                send.wait_recv()
                if relay is not None:
                    relay.start()
            pending.append((out, send))
        if not sign:
            share.wait_recv()
        for relay, started, arriving in relays:
            @pl.when(arriving)
            def _():
                relay.wait_recv()
            pending.append((started, relay))
        pending.append((None, share))
        if sign:
            reflect(w, sign, False)

    def mirror(phase, own, m):
        copies = []
        for i, d in enumerate(sorted(offsets, key=lambda v: -abs(v))):
            c = pltpu.make_async_remote_copy(
                src_ref=own.at[:, (half + d) * b:(half + d + 1) * b],
                dst_ref=m.at[half - d], send_sem=msend.at[phase, i],
                recv_sem=mrecv.at[phase, i], device_id=device(r + d),
                device_id_type=pl.DeviceIdType.MESH)

            @pl.when(valid(d))
            def _():
                c.start()
            copies.append((d, c))
        m[half] = own[:, half * b:(half + 1) * b]
        for d, c in copies:
            @pl.when(valid(-d))
            def _():
                c.wait_recv()
            pending.append((valid(d), c))

    def product(left, w, out):
        for c in range(band):
            lo, hi = max(0, c - half), min(band, c + half + 1)
            rhs = w[pl.ds(pl.multiple_of((core + lo) * b, b), (hi - lo) * b), col(core + 1 + c)]
            acc = jnp.dot(left[:, lo * b:hi * b], rhs, preferred_element_type=jnp.float32)
            keep = present[0, c].astype(jnp.float32)
            out[:, c * b:(c + 1) * b] = (acc * keep).astype(out.dtype)

    def transposed_first():
        for c in range(band):
            lo, hi = max(0, c - half), min(band, c + half + 1)
            rhs = xw[pl.ds(pl.multiple_of((core + c) * b, b), b), col(core + 1 + lo, hi - lo)]
            acc = lax.dot_general(trow[:, lo * b:hi * b], rhs, (((1,), (1,)), ((), ())),
                                  preferred_element_type=jnp.float32)
            keep = present[0, c].astype(jnp.float32)
            cm[:, c * b:(c + 1) * b] = (acc * -keep).astype(cm.dtype)

    stores = []

    def store(src):
        i = len(stores)
        c = pltpu.make_async_copy(src, outs[i].at[0], osem.at[i])
        c.start()
        stores.append(c)

    loads[0].wait()
    spread(0, mv, sw, 1)
    loads[1].wait()
    loads[3].wait()
    product(dv, sw, xrow)
    spread(1, xrow, xw, 0)
    loads[2].wait()
    product(fv, xw, gd)
    store(gd)
    mirror(0, gd, gm.at[0])
    for c in range(band):
        cols = slice(c * b, (c + 1) * b)
        other = gm[0, c].T
        gt[:, cols] = other
        g = gd[:, cols].astype(jnp.float32) - other.astype(jnp.float32)
        trow[:, cols] = (-STEP_SCALE * g).astype(trow.dtype)
    store(gt)
    spread(2, trow, tw, -1, transposed_first)
    product(xrow, tw, cf)
    store(cf)
    store(cm)
    v = cf[...].astype(jnp.float32) + cm[...].astype(jnp.float32)
    ch[...] = v.astype(ch.dtype)
    product(ch, sw, co)
    product(co, tw, qd)
    store(qd)
    mirror(1, qd, gm.at[1])
    for c in range(band):
        qt[:, c * b:(c + 1) * b] = gm[1, c].T
    store(qt)
    for c in stores:
        c.wait()
    for cond, c in pending:
        if cond is None:
            c.wait_send()
        else:
            @pl.when(cond)
            def _():
                c.wait_send()


def local(ncol, n, margin, fock_matrix, density, present):
    rows, b, width = margin.shape
    band = present.shape[1]
    half = (band - 1) // 2
    bf = jnp.bfloat16
    row = pltpu.VMEM((b, width), bf)
    wide = pltpu.VMEM(((band + 1) * b, (band + 3) * b), bf)
    out = jax.ShapeDtypeStruct((rows, b, width), bf)
    outs = pl.pallas_call(
        functools.partial(kernel, ncol, n, b, half),
        out_shape=(out,) * 6,
        in_specs=[pl.BlockSpec(memory_space=pltpu.HBM)] * 4,
        out_specs=[pl.BlockSpec(memory_space=pltpu.HBM)] * 6,
        scratch_shapes=[
            wide, wide, wide, row, row, row, row, row,
            row, row, pltpu.VMEM((2, band, b, b), bf), row, row, row, row, row, row,
            pltpu.SMEM((rows, band), jnp.int32),
            pltpu.SemaphoreType.DMA((4,)),
            pltpu.SemaphoreType.DMA((6,)),
            pltpu.SemaphoreType.DMA((3, 13)),
            pltpu.SemaphoreType.DMA((3, 13)),
            pltpu.SemaphoreType.DMA((2, 2 * half)),
            pltpu.SemaphoreType.DMA((2, 2 * half)),
        ],
        compiler_params=pltpu.CompilerParams(
            collective_id=0, has_side_effects=True, vmem_limit_bytes=67043328),
        name="density_step",
    )(margin, fock_matrix, density, present)
    gd, gt, cf, cm, qd, qt = (v.astype(jnp.float32) for v in outs)
    return gd - gt, density.astype(jnp.float32) + (cf + cm) + 0.5 * (qd + qt)


def solution(mesh):
    nrow, ncol = mesh.shape["row"], mesh.shape["col"]
    spec3 = P(("row", "col"), None, None)
    return jax.shard_map(
        functools.partial(local, ncol, nrow * ncol), mesh=mesh,
        in_specs=(spec3, spec3, spec3, P(("row", "col"), None)),
        out_specs=(spec3, spec3), check_vma=False)
```

```python
import functools

import jax
import jax.numpy as jnp
from jax import lax
from jax.experimental import pallas as pl
from jax.experimental.pallas import tpu as pltpu
from jax.sharding import PartitionSpec as P

STEP_SCALE = 0.015625


def kernel(ncol, n, b, half, margin, fock, density, kept, *rest):
    outs, rest = rest[:5], rest[5:]
    (sw, xw, tw, xrow, trow, dv, fv, mv, gd, gt, gm, cf, cm, ch, co, qd, qt, base, present,
     lsem, osem, wsend, wrecv, msend, mrecv) = rest
    band = 2 * half + 1
    r = lax.axis_index("row") * ncol + lax.axis_index("col")
    k = r // 2
    core = r % 2
    chips = n // 2

    def device(t):
        return {"row": t // ncol, "col": t % ncol}

    def col(i, count=1):
        return pl.ds(pl.multiple_of(i * b, b), count * b)

    def valid_chip(e):
        return jnp.logical_and(k + e >= 0, k + e < chips)

    def valid(d):
        return jnp.logical_and(r + d >= 0, r + d < n)

    sibling = device(r + 1 - 2 * core)
    offsets = [d for d in range(-half, half + 1) if d != 0]
    reach = half // 2
    hops = [e for m in range(1, reach + 1) for e in (m, -m)]

    loads = [
        pltpu.make_async_copy(margin.at[0], mv, lsem.at[0]),
        pltpu.make_async_copy(density.at[0], dv, lsem.at[1]),
        pltpu.make_async_copy(fock.at[0], fv, lsem.at[2]),
        pltpu.make_async_copy(kept, present, lsem.at[3]),
    ]
    for c in loads:
        c.start()

    barrier = pltpu.get_barrier_semaphore()
    for d in offsets:
        @pl.when(valid(d))
        def _():
            pl.semaphore_signal(barrier, inc=1, device_id=device(r + d),
                                device_id_type=pl.DeviceIdType.MESH)

    for e in hops:
        @pl.when(jnp.logical_not(valid_chip(e)))
        def _():
            p = half + 2 * e
            for w in (sw, xw, tw):
                w[p * b:(p + 2) * b, :] = jnp.zeros((2 * b, w.shape[1]), w.dtype)
    for d in offsets:
        @pl.when(jnp.logical_not(valid(-d)))
        def _():
            for m in (gm.at[0], gm.at[1]):
                m[half - d] = jnp.zeros((b, b), gm.dtype)

    expected = jnp.minimum(r, half) + jnp.minimum(n - 1 - r, half)
    pl.semaphore_wait(barrier, expected)

    pending = []

    def window_plan(symmetric, c):
        plan = []
        for e in hops:
            m = abs(e)
            p = half - 2 * e + c
            if not symmetric:
                lo, hi = max(0, p - half), min(band, p + half)
                plan.append((e, p, lo, hi - lo + 1))
            elif e > 0:
                plan.append((e, p, 0, p + 1))
                if m == 1 and c == 1:
                    plan.append((e, p, half + 2, 2))
            else:
                plan.append((e, p, p, band + 1 - p))
                if m == 1 and c == 0:
                    plan.append((e, p, half - 2, 1))
        return plan

    def known_blocks():
        return {(p, j) for c in (0, 1) for _, p, lo, count in window_plan(True, c)
                for j in range(lo, lo + count)}

    def reflect(w, sign, own_rows):
        known = known_blocks()
        middle = (half, half + 1)
        for i in range(band + 1):
            for j in range(band + 1):
                if abs(i - j) > half or i in middle or (i, j) in known:
                    continue
                if (j in middle) != own_rows:
                    continue
                block = w[j * b:(j + 1) * b, (i + 1) * b:(i + 2) * b].T
                w[i * b:(i + 1) * b, (j + 1) * b:(j + 2) * b] = block if sign > 0 else -block

    def both(x, y):
        return jnp.logical_and(x, y)

    def spread(phase, own, w, sign, beside=None):
        here = pl.ds(pl.multiple_of((half + core) * b, b), b)
        sends, relays = [], []
        for cc in (0, 1):
            mine, theirs = core == cc, core == 1 - cc
            for i, (e, p, lo, count) in enumerate(window_plan(sign != 0, cc)):
                spot = w.at[p * b:(p + 1) * b, (lo + 1) * b:(lo + 1 + count) * b]
                s0 = lo - p + half
                send = pltpu.make_async_remote_copy(
                    src_ref=own.at[:, s0 * b:(s0 + count) * b], dst_ref=spot,
                    send_sem=wsend.at[phase, i], recv_sem=wrecv.at[phase, i],
                    device_id=device(r + 2 * e), device_id_type=pl.DeviceIdType.MESH)
                out, back = both(mine, valid_chip(e)), both(mine, valid_chip(-e))
                relay = None
                if 0 < p < band:
                    relay = pltpu.make_async_remote_copy(
                        src_ref=spot, dst_ref=spot, send_sem=wsend.at[phase, 6 + i],
                        recv_sem=wrecv.at[phase, 6 + i], device_id=sibling,
                        device_id_type=pl.DeviceIdType.MESH)
                    relays.append((relay, back, both(theirs, valid_chip(-e))))

                @pl.when(out)
                def _():
                    send.start()
                sends.append((send, relay, out, back))
        share = pltpu.make_async_remote_copy(
            src_ref=own, dst_ref=w.at[here, col(core + 1, band)],
            send_sem=wsend.at[phase, 12], recv_sem=wrecv.at[phase, 12],
            device_id=sibling, device_id_type=pl.DeviceIdType.MESH)
        share.start()
        w[here, col(core + 1, band)] = own[...]
        if sign:
            share.wait_recv()
            reflect(w, sign, True)
        if beside is not None:
            beside()
        for send, relay, out, back in sends:
            @pl.when(back)
            def _():
                send.wait_recv()
                if relay is not None:
                    relay.start()
            pending.append((out, send))
        if not sign:
            share.wait_recv()
        for relay, started, arriving in relays:
            @pl.when(arriving)
            def _():
                relay.wait_recv()
            pending.append((started, relay))
        pending.append((None, share))
        if sign:
            reflect(w, sign, False)

    def mirror(phase, left, w, own, m):
        product(left, w, own, (half,))
        copies = []
        for i, d in enumerate(sorted(offsets, key=lambda v: -abs(v))):
            product(left, w, own, (half + d,))
            c = pltpu.make_async_remote_copy(
                src_ref=own.at[:, (half + d) * b:(half + d + 1) * b],
                dst_ref=m.at[half - d], send_sem=msend.at[phase, i],
                recv_sem=mrecv.at[phase, i], device_id=device(r + d),
                device_id_type=pl.DeviceIdType.MESH)

            @pl.when(valid(d))
            def _():
                c.start()
            copies.append((d, c))
        m[half] = own[:, half * b:(half + 1) * b]
        for d, c in copies:
            @pl.when(valid(-d))
            def _():
                c.wait_recv()
            pending.append((valid(d), c))

    def product(left, w, out, columns=None):
        for c in columns or range(band):
            lo, hi = max(0, c - half), min(band, c + half + 1)
            rhs = w[pl.ds(pl.multiple_of((core + lo) * b, b), (hi - lo) * b), col(core + 1 + c)]
            acc = jnp.dot(left[:, lo * b:hi * b], rhs, preferred_element_type=jnp.float32)
            keep = present[0, c].astype(jnp.float32)
            out[:, c * b:(c + 1) * b] = (acc * keep).astype(out.dtype)

    def transposed_first():
        for c in range(band):
            lo, hi = max(0, c - half), min(band, c + half + 1)
            rhs = xw[pl.ds(pl.multiple_of((core + c) * b, b), b), col(core + 1 + lo, hi - lo)]
            acc = lax.dot_general(trow[:, lo * b:hi * b], rhs, (((1,), (1,)), ((), ())),
                                  preferred_element_type=jnp.float32)
            keep = present[0, c].astype(jnp.float32)
            cm[:, c * b:(c + 1) * b] = (acc * -keep).astype(cm.dtype)

    stores = []

    def store(src):
        i = len(stores)
        c = pltpu.make_async_copy(src, outs[i].at[0], osem.at[i])
        c.start()
        stores.append(c)

    loads[0].wait()
    spread(0, mv, sw, 1)
    loads[1].wait()
    loads[3].wait()
    product(dv, sw, xrow)
    spread(1, xrow, xw, 0)
    loads[2].wait()
    mirror(0, fv, xw, gd, gm.at[0])
    store(gd)
    for c in range(band):
        cols = slice(c * b, (c + 1) * b)
        other = gm[0, c].T
        gt[:, cols] = other
        g = gd[:, cols].astype(jnp.float32) - other.astype(jnp.float32)
        trow[:, cols] = (-STEP_SCALE * g).astype(trow.dtype)
    store(gt)
    spread(2, trow, tw, -1, transposed_first)
    product(xrow, tw, cf)
    v = cf[...].astype(jnp.float32) + cm[...].astype(jnp.float32)
    ch[...] = v.astype(ch.dtype)
    base[...] = dv[...].astype(jnp.float32) + v
    store(base)
    product(ch, sw, co)
    mirror(1, co, tw, qd, gm.at[1])
    store(qd)
    for c in range(band):
        qt[:, c * b:(c + 1) * b] = gm[1, c].T
    store(qt)
    for c in stores:
        c.wait()
    for cond, c in pending:
        if cond is None:
            c.wait_send()
        else:
            @pl.when(cond)
            def _():
                c.wait_send()


def local(ncol, n, margin, fock_matrix, density, present):
    rows, b, width = margin.shape
    band = present.shape[1]
    half = (band - 1) // 2
    bf = jnp.bfloat16
    row = pltpu.VMEM((b, width), bf)
    wide = pltpu.VMEM(((band + 1) * b, (band + 3) * b), bf)
    out = jax.ShapeDtypeStruct((rows, b, width), bf)
    outs = pl.pallas_call(
        functools.partial(kernel, ncol, n, b, half),
        out_shape=(out, out, jax.ShapeDtypeStruct((rows, b, width), jnp.float32), out, out),
        in_specs=[pl.BlockSpec(memory_space=pltpu.HBM)] * 4,
        out_specs=[pl.BlockSpec(memory_space=pltpu.HBM)] * 5,
        scratch_shapes=[
            wide, wide, wide, row, row, row, row, row,
            row, row, pltpu.VMEM((2, band, b, b), bf), row, row, row, row, row, row,
            pltpu.VMEM((b, width), jnp.float32), pltpu.SMEM((rows, band), jnp.int32),
            pltpu.SemaphoreType.DMA((4,)),
            pltpu.SemaphoreType.DMA((5,)),
            pltpu.SemaphoreType.DMA((3, 13)),
            pltpu.SemaphoreType.DMA((3, 13)),
            pltpu.SemaphoreType.DMA((2, 2 * half)),
            pltpu.SemaphoreType.DMA((2, 2 * half)),
        ],
        compiler_params=pltpu.CompilerParams(
            collective_id=0, has_side_effects=True, vmem_limit_bytes=67043328),
        name="density_step",
    )(margin, fock_matrix, density, present)
    gd, gt, base, qd, qt = (v.astype(jnp.float32) for v in outs)
    return gd - gt, base + 0.5 * (qd + qt)


def solution(mesh):
    nrow, ncol = mesh.shape["row"], mesh.shape["col"]
    spec3 = P(("row", "col"), None, None)
    return jax.shard_map(
        functools.partial(local, ncol, nrow * ncol), mesh=mesh,
        in_specs=(spec3, spec3, spec3, P(("row", "col"), None)),
        out_specs=(spec3, spec3), check_vma=False)
```
